32 devices in a mesh: dp: 32 (over z, y, x, core).
Axes of the slice: x: 2, y: 2, z: 4, core: 2. Of those that a mesh axis runs over, the one named last changes fastest.
Arguments:
- tokens: bfloat16 [64, 1024, 768], P(None, 'dp'), may hold values from -6 to 6
- cotangent: bfloat16 [64, 1024, 768], P(None, 'dp'), may hold values from -6 to 6
- lengths: int32 [64], replicated, may hold values from 1 to 1024, 32768 in all
- order: int32 [64], replicated, may hold values from 0 to 63, each once
- query_weight: bfloat16 [768, 768], P('dp'), may hold values from -0.21875 to 0.21875
- query_bias: bfloat16 [768], P('dp'), may hold values from -3 to 3
- key_weight: bfloat16 [768, 768], P('dp'), may hold values from -0.21875 to 0.21875
- value_weight: bfloat16 [768, 768], P('dp'), may hold values from -0.21875 to 0.21875
- value_bias: bfloat16 [768], P('dp'), may hold values from -3 to 3
- output_weight: bfloat16 [768, 768], P('dp'), may hold values from -1.75 to 1.75
- output_bias: bfloat16 [768], P('dp'), may hold values from -3 to 3
- first_gain: bfloat16 [768], P('dp'), may hold values from 0.5 to 1.5
- first_shift: bfloat16 [768], P('dp'), may hold values from -3 to 3
- inner_weight: bfloat16 [768, 3072], P('dp'), may hold values from -0.21875 to 0.21875
- inner_bias: bfloat16 [3072], P('dp'), may hold values from -3 to 3
- outer_weight: bfloat16 [3072, 768], P('dp'), may hold values from -0.109375 to 0.109375
- outer_bias: bfloat16 [768], P('dp'), may hold values from -3 to 3
- second_gain: bfloat16 [768], P('dp'), may hold values from 0.5 to 1.5
- second_shift: bfloat16 [768], P('dp'), may hold values from -3 to 3
Outputs:
- output: bfloat16 [64, 1024, 768], P(None, 'dp')
- input_gradient: bfloat16 [64, 1024, 768], P(None, 'dp')
- query_weight_gradient: float32 [768, 768], P('dp')
- query_bias_gradient: float32 [768], P('dp')
- key_weight_gradient: float32 [768, 768], P('dp')
- value_weight_gradient: float32 [768, 768], P('dp')
- value_bias_gradient: float32 [768], P('dp')
- output_weight_gradient: float32 [768, 768], P('dp')
- output_bias_gradient: float32 [768], P('dp')
- first_gain_gradient: float32 [768], P('dp')
- first_shift_gradient: float32 [768], P('dp')
- inner_weight_gradient: float32 [768, 3072], P('dp')
- inner_bias_gradient: float32 [3072], P('dp')
- outer_weight_gradient: float32 [3072, 768], P('dp')
- outer_bias_gradient: float32 [768], P('dp')
- second_gain_gradient: float32 [768], P('dp')
- second_shift_gradient: float32 [768], P('dp')
The draws below stay inside these ranges and needn't reach their ends.
Inputs may be any that keep to these rules, and one draw needn't show every extreme that they name: The lengths add up to 32768, and some sequence has exactly 1024 tokens. `order`: every sequence number appears once; slots k * 2 to (k + 1) * 2 - 1 belong to device k.
All inputs are finite; a program needn't handle non-finite values.
Results may differ from the reference program's by a relative error of at most 0.015.
Values may be sent and summed in bfloat16 or wider, within the bound.
A program may use at most 448 MiB of HBM per device.

```python
import math
import jax
import jax.numpy as jnp
import numpy as np
from jax import lax

D = 768
HEADS = 12
HEAD = 64
FF = 3072
LMAX = 1024
NSEQ = 64


def shard_levels(stream_key, dims, cuts, smallest, high):
    factor_of = 1.0
    for position, shards_of in cuts:
        steps = jax.random.uniform(jax.random.fold_in(jax.random.fold_in(stream_key, 6), position), (shards_of,), jnp.float32, smallest / len(cuts), high / len(cuts))
        factor_of = factor_of * jnp.repeat(jnp.exp(steps), dims[position] // shards_of).reshape((-1,) + (1,) * (len(dims) - 1 - position))
    return factor_of


def length_profile(number_of, total, limit, slope):
    weights = [(1 << 20) // math.isqrt(rank ** slope) + 1 for rank in range(2, number_of + 1)]
    rest, given = total - limit - (number_of - 1), [1] * (number_of - 1)
    while rest > 0:
        free = [i for i in range(number_of - 1) if given[i] < limit]
        pool, budget = sum([weights[i] for i in free]), rest
        for i in free:
            more = min(limit - given[i], max(1, budget * weights[i] // pool), rest)
            given[i] = given[i] + more
            rest = rest - more
    return np.array([limit] + given)


def uneven_parts(rng, amount, total, bound, slope):
    if amount == 2:
        one = jax.random.randint(rng, (), max(1, total - bound), min(bound, total - 1) + 1)
        return jnp.stack([one, total - one])
    tallies = jnp.asarray(length_profile(amount, total, bound, slope), jnp.int32)
    twos = (amount - 1) // 2
    source_of, taker = tallies[1:1 + 2 * twos:2], tallies[2:2 + 2 * twos:2]
    margin = jnp.minimum(source_of - 1, bound - taker)
    moved = jax.random.randint(jax.random.fold_in(rng, 1), (twos,), 0, 1 << 20) % (margin + 1)
    tallies = tallies.at[1:1 + 2 * twos:2].set(source_of - moved).at[2:2 + 2 * twos:2].set(taker + moved)
    return tallies[jax.random.permutation(jax.random.fold_in(rng, 2), amount)]


def bell_draw(stream_key, shape, width, reach, split=(), held_as=jnp.bfloat16):
    factor_of = shard_levels(stream_key, shape, split, -0.22, 0.18) if split else 1.0
    entries = jax.random.normal(stream_key, shape, jnp.float32) * width * factor_of
    return jnp.minimum(jnp.maximum(entries, -reach), reach).astype(held_as)


def setup_inputs(seed: int = 0) -> dict:
    key_list = jax.random.split(jax.random.key(seed), 20)
    tokens = bell_draw(key_list[0], (NSEQ, LMAX, D), 1.0, 6.0, ((1, 32),))
    cotangent = bell_draw(key_list[1], (NSEQ, LMAX, D), 1.0, 6.0, ((1, 32),))
    lengths = uneven_parts(key_list[2], NSEQ, NSEQ * LMAX // 2, LMAX, 2).astype(jnp.int32)
    order = jax.random.permutation(key_list[3], NSEQ).astype(jnp.int32)
    query_weight = bell_draw(key_list[4], (D, D), D ** -0.5, 0.21875, ((0, 32),))
    query_bias = bell_draw(key_list[5], (D,), 0.5, 3.0, ((0, 32),))
    key_weight = bell_draw(key_list[6], (D, D), D ** -0.5, 0.21875, ((0, 32),))
    value_weight = bell_draw(key_list[7], (D, D), D ** -0.5, 0.21875, ((0, 32),))
    value_bias = bell_draw(key_list[8], (D,), 0.5, 3.0, ((0, 32),))
    output_weight = bell_draw(key_list[9], (D, D), (D // 64) ** -0.5, 1.75, ((0, 32),))
    output_bias = bell_draw(key_list[10], (D,), 0.5, 3.0, ((0, 32),))
    first_gain = jnp.clip(1.0 + 0.1 * jax.random.normal(key_list[11], (D,), jnp.float32), 0.5, 1.5).astype(jnp.bfloat16)
    first_shift = bell_draw(key_list[12], (D,), 0.5, 3.0, ((0, 32),))
    inner_weight = bell_draw(key_list[13], (D, FF), D ** -0.5, 0.21875, ((0, 32),))
    inner_bias = bell_draw(key_list[14], (FF,), 0.5, 3.0, ((0, 32),))
    outer_weight = bell_draw(key_list[15], (FF, D), FF ** -0.5, 0.109375, ((0, 32),))
    outer_bias = bell_draw(key_list[16], (D,), 0.5, 3.0, ((0, 32),))
    second_gain = jnp.clip(1.0 + 0.1 * jax.random.normal(key_list[17], (D,), jnp.float32), 0.5, 1.5).astype(jnp.bfloat16)
    second_shift = bell_draw(key_list[18], (D,), 0.5, 3.0, ((0, 32),))
    return dict(tokens=tokens, cotangent=cotangent, lengths=lengths, order=order, query_weight=query_weight, query_bias=query_bias, key_weight=key_weight, value_weight=value_weight, value_bias=value_bias, output_weight=output_weight, output_bias=output_bias, first_gain=first_gain, first_shift=first_shift, inner_weight=inner_weight, inner_bias=inner_bias, outer_weight=outer_weight, outer_bias=outer_bias, second_gain=second_gain, second_shift=second_shift)


@jax.custom_vjp
def low(v):
    return lax.optimization_barrier(v.astype(jnp.bfloat16)).astype(jnp.float32)

@jax.custom_vjp
def low_back(v):
    return v

def low_keep(v):
    return (low(v), None)

def low_pass(kept, grad):
    return (grad,)

def back_keep(v):
    return (v, None)

def back_low(kept, grad):
    return (low(grad),)
low.defvjp(low_keep, low_pass)
low_back.defvjp(back_keep, back_low)
epsilon = 1e-05
highest = lax.Precision.HIGHEST

def matmul(left, right):
    return jnp.dot(left, right, precision=highest)

def layer_norm(hidden, gain, shift):
    center = hidden - lax.optimization_barrier(jnp.mean(hidden, axis=-1, keepdims=True))
    scale = lax.rsqrt(lax.optimization_barrier(jnp.mean(center * center, axis=-1, keepdims=True)) + epsilon)
    return center * scale * gain + shift

def one_sequence(params, rows, length):
    query_weight, query_bias, key_weight, value_weight, value_bias, output_weight, output_bias, first_gain, first_shift, inner_weight, inner_bias, outer_weight, outer_bias, second_gain, second_shift = params
    inputs = low(rows)
    queries = low_back(low(matmul(inputs, query_weight) + query_bias)).reshape(LMAX, HEADS, HEAD)
    keys = low_back(low(matmul(inputs, key_weight))).reshape(LMAX, HEADS, HEAD)
    values = low_back(low(matmul(inputs, value_weight) + value_bias)).reshape(LMAX, HEADS, HEAD)
    scores = low_back(jnp.einsum('qhd,khd->hqk', queries, keys, precision=highest) * HEAD ** (-0.5))
    keep = jnp.arange(LMAX) < length
    probs = jax.nn.softmax(jnp.where(keep[None, None, :], scores, -1e+30), axis=-1)
    context = jnp.einsum('hqk,khd->qhd', low(probs), values, precision=highest)
    context = low_back(low(context)).reshape(LMAX, D)
    attended = low_back(matmul(context, output_weight) + output_bias)
    mixed = layer_norm(rows + attended, first_gain, first_shift)
    inner = low_back(matmul(low(mixed), inner_weight) + inner_bias)
    activated = low(jax.nn.gelu(inner, approximate=False))
    branch = low_back(matmul(activated, outer_weight) + outer_bias)
    result = layer_norm(mixed + branch, second_gain, second_shift)
    return result * keep[:, None]

def reference(tokens, cotangent, lengths, order, query_weight, query_bias, key_weight, value_weight, value_bias, output_weight, output_bias, first_gain, first_shift, inner_weight, inner_bias, outer_weight, outer_bias, second_gain, second_shift):
    params = tuple((w.astype(jnp.float32) for w in (query_weight, query_bias, key_weight, value_weight, value_bias, output_weight, output_bias, first_gain, first_shift, inner_weight, inner_bias, outer_weight, outer_bias, second_gain, second_shift)))
    dealt = jnp.take(tokens, order, axis=0).astype(jnp.float32)
    dealt_lengths = jnp.take(lengths, order)

    def forward(weights, rows):

        def single(item):
            return jax.checkpoint(one_sequence)(weights, item[0], item[1])
        return lax.map(single, (rows, dealt_lengths))
    output, pullback = jax.vjp(forward, params, dealt)
    weight_grads, input_grad = pullback(cotangent.astype(jnp.float32))
    grad_qw, grad_qb, grad_kw, grad_vw, grad_vb, grad_ow, grad_ob, grad_fg, grad_fs, grad_iw, grad_ib, grad_uw, grad_ub, grad_sg, grad_ss = weight_grads
    return (output.astype(jnp.bfloat16), input_grad.astype(jnp.bfloat16), grad_qw, grad_qb, grad_kw, grad_vw, grad_vb, grad_ow, grad_ob, grad_fg, grad_fs, grad_iw, grad_ib, grad_uw, grad_ub, grad_sg, grad_ss)
```

```python
import functools
import math

import jax
import jax.numpy as jnp
from jax import lax
from jax.experimental import pallas as pl
from jax.experimental.pallas import tpu as pltpu
from jax.sharding import PartitionSpec as P

F32 = jnp.float32
BF16 = jnp.bfloat16
MESH = pl.DeviceIdType.MESH
ANY = pl.BlockSpec(memory_space=pl.ANY)

HEADS = 12
D = 768
FF = 3072
WIDE = 3 * D
T = 1024
SUB = 32
B = 256
RP = 2816
SLOTS = 4
EPS = 1e-05
LOG2E = 1.4426950408889634
SCALE = 64 ** (-0.5)
SC2 = SCALE * LOG2E

GROUP_PLANE = (2, 3, 1, 0, 0, 1, 0, 0)
GROUP_SLOT = (0, 0, 0, 0, 1, 1, 2, 3)
GROUP_TURN = (False, False, False, False, True, True, False, True)
CAPS = (
    (4, 4, 4, 3, 2, 2, 1, 1),
    (4, 4, 4, 3, 2, 2, 2, 2),
    (4, 4, 4, 4, 4, 4, 4, 4),
)


def dot(left, right):
    return jnp.dot(left, right, preferred_element_type=F32)


def dot_nt(left, right):
    return lax.dot_general(left, right, (((1,), (1,)), ((), ())), preferred_element_type=F32)


def dot_tn(left, right):
    return lax.dot_general(left, right, (((0,), (0,)), ((), ())), preferred_element_type=F32)


def al(x, k):
    return pl.multiple_of(x, k)


def group_device(g, i, quarter):
    place = (quarter - 1 - i) if GROUP_TURN[g] else i
    return GROUP_PLANE[g] * quarter + place


def plane_groups(plane):
    return [g for g in range(8) if GROUP_PLANE[g] == plane]


def sort_kernel(seq_ref, slot_ref, tok, cot, tok_o, cot_o, sem):
    count = tok.shape[0]

    def copies(r):
        return (
            pltpu.make_async_copy(tok.at[seq_ref[r]], tok_o.at[r], sem.at[0]),
            pltpu.make_async_copy(cot.at[slot_ref[r]], cot_o.at[r], sem.at[1]),
        )

    def start(r, _):
        for c in copies(r):
            c.start()
        return 0

    def wait(r, _):
        for c in copies(r):
            c.wait()
        return 0

    lax.fori_loop(0, count, start, 0)
    lax.fori_loop(0, count, wait, 0)


def sort_blocks(seq_of_rank, slot_of_rank, tokens, cotangent):
    return pl.pallas_call(
        sort_kernel,
        grid_spec=pltpu.PrefetchScalarGridSpec(
            num_scalar_prefetch=2,
            grid=(),
            in_specs=[ANY, ANY],
            out_specs=[ANY, ANY],
            scratch_shapes=[pltpu.SemaphoreType.DMA((2,))],
        ),
        out_shape=[jax.ShapeDtypeStruct(tokens.shape, BF16)] * 2,
        name="sort_blocks",
    )(seq_of_rank, slot_of_rank, tokens, cotangent)


def unsort_kernel(rank_ref, live_ref, y, o, zero, sem):
    count = o.shape[0]
    zero[...] = jnp.zeros_like(zero)

    def start(j, _):
        @pl.when(live_ref[j] > 0)
        def _():
            pltpu.make_async_copy(y.at[rank_ref[j]], o.at[j], sem.at[0]).start()

        @pl.when(live_ref[j] <= 0)
        def _():
            pltpu.make_async_copy(zero, o.at[j], sem.at[0]).start()

        return 0

    def wait(j, _):
        pltpu.make_async_copy(zero, o.at[j], sem.at[0]).wait()
        return 0

    lax.fori_loop(0, count, start, 0)
    lax.fori_loop(0, count, wait, 0)


def unsort_blocks(rank_of_slot, live, y):
    return pl.pallas_call(
        unsort_kernel,
        grid_spec=pltpu.PrefetchScalarGridSpec(
            num_scalar_prefetch=2,
            grid=(),
            in_specs=[ANY],
            out_specs=ANY,
            scratch_shapes=[pltpu.VMEM(y.shape[1:], BF16), pltpu.SemaphoreType.DMA((1,))],
        ),
        out_shape=jax.ShapeDtypeStruct(y.shape, BF16),
        name="unsort_blocks",
    )(rank_of_slot, live, y)


def meet(n):
    me = lax.axis_index("dp")
    barrier = pltpu.get_barrier_semaphore()

    def signal(k, _):
        pl.semaphore_signal(barrier, inc=1, device_id=(lax.rem(me + k, n),), device_id_type=MESH)
        return 0

    lax.fori_loop(1, n, signal, 0)
    pl.semaphore_wait(barrier, n - 1)


def deal_kernel(n, caps, x, o, send, recv):
    quarter = n // 4
    rows = x.shape[1]
    me = lax.axis_index("dp")
    plane = me // quarter
    meet(n)
    for g in range(8):
        slot = GROUP_SLOT[g]
        place = o.at[slot, pl.ds(al(me * rows, 8), rows)]

        def start(i, _, g=g, slot=slot, place=place):
            to = group_device(g, i, quarter)
            block = x.at[g * quarter + i]

            @pl.when(to == me)
            def _():
                pltpu.make_async_copy(block, place, recv.at[slot]).start()

            @pl.when(to != me)
            def _():
                pltpu.make_async_remote_copy(
                    block, place, send, recv.at[slot], device_id=(to,), device_id_type=MESH
                ).start()

            return 0

        @pl.when(plane < caps[g])
        def _(start=start):
            lax.fori_loop(0, quarter, start, 0)

    for p in range(4):
        mine = plane_groups(p)
        sent = sum(quarter for g in range(8) if p < caps[g]) - sum(1 for g in mine if p < caps[g])

        @pl.when(plane == p)
        def _(mine=mine, sent=sent):
            for g in mine:
                slot = GROUP_SLOT[g]
                whole = o.at[slot, pl.ds(0, caps[g] * quarter * rows)]
                pltpu.make_async_copy(whole, whole, recv.at[slot]).wait()
            if sent:
                pltpu.make_async_copy(x.at[pl.ds(0, sent)], x.at[pl.ds(0, sent)], send).wait()


def deal(x, n, caps, collective_id):
    return pl.pallas_call(
        functools.partial(deal_kernel, n, caps),
        in_specs=[ANY],
        out_specs=ANY,
        out_shape=jax.ShapeDtypeStruct((SLOTS, T, D), BF16),
        scratch_shapes=[pltpu.SemaphoreType.DMA, pltpu.SemaphoreType.DMA((SLOTS,))],
        compiler_params=pltpu.CompilerParams(collective_id=collective_id, has_side_effects=True),
        name="deal",
    )(x)


def collect_kernel(n, caps, x, o, send, recv):
    quarter = n // 4
    rows = o.shape[1]
    me = lax.axis_index("dp")
    plane = me // quarter
    place = lax.rem(me, quarter)
    meet(n)
    for p in range(4):

        @pl.when(plane == p)
        def _(p=p):
            for g in plane_groups(p):
                slot = GROUP_SLOT[g]
                i = (quarter - 1 - place) if GROUP_TURN[g] else place
                rank = g * quarter + i

                def start(k, _, slot=slot, rank=rank):
                    block = x.at[slot, pl.ds(al(k * rows, 8), rows)]

                    @pl.when(k == me)
                    def _():
                        pltpu.make_async_copy(block, o.at[rank], recv).start()

                    @pl.when(k != me)
                    def _():
                        pltpu.make_async_remote_copy(
                            block, o.at[rank], send, recv, device_id=(k,), device_id_type=MESH
                        ).start()

                    return 0

                lax.fori_loop(0, caps[g] * quarter, start, 0)

    for p in range(4):
        mine = plane_groups(p)
        got = sum(quarter for g in range(8) if p < caps[g])
        sent = sum(caps[g] * quarter for g in mine) - sum(1 for g in mine if p < caps[g])

        @pl.when(plane == p)
        def _(got=got, sent=sent):
            whole = o.at[pl.ds(0, got)]
            pltpu.make_async_copy(whole, whole, recv).wait()
            left = sent
            for slot in range(SLOTS):
                now = min(left, n)
                if now:
                    part = x.at[slot, pl.ds(0, now * rows)]
                    pltpu.make_async_copy(part, part, send).wait()
                left -= now


def collect(x, n, nseq, rows, caps, collective_id):
    return pl.pallas_call(
        functools.partial(collect_kernel, n, caps),
        in_specs=[ANY],
        out_specs=ANY,
        out_shape=jax.ShapeDtypeStruct((nseq, rows, D), BF16),
        scratch_shapes=[pltpu.SemaphoreType.DMA, pltpu.SemaphoreType.DMA],
        compiler_params=pltpu.CompilerParams(collective_id=collective_id, has_side_effects=True),
        name="collect",
    )(x)


def attend_kernel(
    lens, offs, tot, x, w, bias, rows_o, qkv_o, ctx_o, lse_o, rows_v, qkv_v, ctx_v, lse_v, sem_in, sem_out
):
    total = al(tot[0], SUB)
    blocks = tot[1]

    def pieces(act):
        for s in range(SLOTS):
            off = offs[s]

            def one(j, _, s=s, off=off):
                act(
                    pltpu.make_async_copy(
                        x.at[s, pl.ds(al(j * SUB, SUB), SUB)],
                        rows_v.at[pl.ds(al(off + j * SUB, SUB), SUB)],
                        sem_in,
                    )
                )
                return 0

            lax.fori_loop(0, (lens[s] + SUB - 1) // SUB, one, 0)

    pieces(lambda c: c.start())
    rows_v[pl.ds(total, B), :] = jnp.zeros((B, D), BF16)
    qkv_v[pl.ds(al(blocks * B, B), B), :] = jnp.zeros((B, WIDE), BF16)
    pieces(lambda c: c.wait())

    def outs(b):
        at = pl.ds(al(b * B, B), B)
        return (
            pltpu.make_async_copy(rows_v.at[at], rows_o.at[at], sem_out.at[0]),
            pltpu.make_async_copy(qkv_v.at[at], qkv_o.at[at], sem_out.at[1]),
        )

    def project(b, _):
        at = pl.ds(al(b * B, B), B)
        for part in range(3):
            cols = slice(part * D, (part + 1) * D)
            qkv_v[at, cols] = (dot(rows_v[at, :], w[:, cols]) + bias[:, cols]).astype(BF16)
        for c in outs(b):
            c.start()
        return 0

    lax.fori_loop(0, blocks, project, 0)

    lane = lax.broadcasted_iota(jnp.int32, (B, 128), 1)
    column = lax.broadcasted_iota(jnp.int32, (B, B), 1)

    def sequence(s, _):
        length = lens[s]
        off = offs[s]
        spans = (length + B - 1) // B

        def attend(q, t):
            r0 = al(off + q * B, SUB)

            def pair(p, lse):
                c0 = al(p * 128, 128)
                qp = qkv_v[pl.ds(r0, B), pl.ds(c0, 128)]
                ks = [qkv_v[pl.ds(al(off + j * B, SUB), B), pl.ds(al(D + p * 128, 128), 128)] for j in range(t)]
                vs = [qkv_v[pl.ds(al(off + j * B, SUB), B), pl.ds(al(2 * D + p * 128, 128), 128)] for j in range(t)]
                done = []
                for h in range(2):
                    half = (lane < 64) if h == 0 else (lane >= 64)
                    qm = jnp.where(half, qp, jnp.zeros_like(qp))
                    ss = [dot_nt(qm, k) for k in ks]
                    ss[-1] = jnp.where(column < length - (t - 1) * B, ss[-1], -1e30)
                    top = functools.reduce(jnp.maximum, ss)
                    top = jnp.max(top, axis=1, keepdims=True)
                    ps = [jnp.exp2((sc - top) * SC2) for sc in ss]
                    summed = jnp.sum(functools.reduce(jnp.add, ps), axis=1, keepdims=True)
                    o = functools.reduce(jnp.add, [dot(pr.astype(BF16), v) for pr, v in zip(ps, vs)])
                    done.append(o * (1.0 / summed))
                    lse = jnp.where(lane == 2 * p + h, top * SC2 + jnp.log(summed) * LOG2E, lse)
                ctx_v[pl.ds(r0, B), pl.ds(c0, 128)] = jnp.where(lane < 64, done[0], done[1]).astype(BF16)
                return lse

            lse_v[pl.ds(r0, B), :] = lax.fori_loop(0, HEADS // 2, pair, jnp.zeros((B, 128), F32))

        def query_block(q, _):
            for t in range(1, T // B + 1):

                @pl.when(spans == t)
                def _(t=t):
                    attend(q, t)

            return 0

        lax.fori_loop(0, spans, query_block, 0)
        return 0

    lax.fori_loop(0, SLOTS, sequence, 0)
    ctx_v[pl.ds(total, B), :] = jnp.zeros((B, D), BF16)

    def more(b):
        at = pl.ds(al(b * B, B), B)
        return (
            pltpu.make_async_copy(ctx_v.at[at], ctx_o.at[at], sem_out.at[2]),
            pltpu.make_async_copy(lse_v.at[at], lse_o.at[at], sem_out.at[3]),
        )

    def start_more(b, _):
        for c in more(b):
            c.start()
        return 0

    def finish(b, _):
        for c in outs(b) + more(b):
            c.wait()
        return 0

    lax.fori_loop(0, blocks, start_more, 0)
    lax.fori_loop(0, blocks, finish, 0)


def attend(lens, offs, tot, x, w, bias):
    shapes = [((RP, D), BF16), ((RP, WIDE), BF16), ((RP, D), BF16), ((RP, 128), F32)]
    return pl.pallas_call(
        attend_kernel,
        grid_spec=pltpu.PrefetchScalarGridSpec(
            num_scalar_prefetch=3,
            grid=(),
            in_specs=[ANY, pl.BlockSpec(memory_space=pltpu.VMEM), pl.BlockSpec(memory_space=pltpu.VMEM)],
            out_specs=[ANY] * 4,
            scratch_shapes=[pltpu.VMEM(s, d) for s, d in shapes]
            + [pltpu.SemaphoreType.DMA, pltpu.SemaphoreType.DMA((4,))],
        ),
        out_shape=[jax.ShapeDtypeStruct(s, d) for s, d in shapes],
        compiler_params=pltpu.CompilerParams(vmem_limit_bytes=60 << 20),
        name="attend",
    )(lens, offs, tot, x, w, bias)


def live_mask(live, b):
    row = lax.broadcasted_iota(jnp.int32, (B, 1), 0)
    keep = None
    for k in range(B // SUB):
        here = (row >= k * SUB) & (row < k * SUB + live[b * (B // SUB) + k])
        keep = here if keep is None else keep | here
    return keep


def norm(hidden):
    center = hidden - jnp.mean(hidden, axis=-1, keepdims=True)
    scale = lax.rsqrt(jnp.mean(center * center, axis=-1, keepdims=True) + EPS)
    return center * scale, scale


def norm_back(e, normed, scale):
    first = jnp.mean(e, axis=-1, keepdims=True)
    second = jnp.mean(e * normed, axis=-1, keepdims=True)
    return scale * (e - first - normed * second)


def rows_kernel(
    tot, sslot, spos, live, *refs
):
    @pl.when(pl.program_id(0) < tot[1])
    def _():
        rows_block(tot, sslot, spos, live, *refs)


def rows_block(
    tot, sslot, spos, live, rows, ctx, cot, wo, wi, wu, vec, bi,
    out_o, ga_o, gc_o, dd_o, gwo_o, gwi_o, gwu_o, gvec_o, gbi_o,
    cot_v, out_v, act_v, dg_v, gwo, gwi, gwu, gvec, gbi, stage, sem_c, sem_o, sem_w,
):
    b = pl.program_id(0)
    nb = tot[1]
    subs = B // SUB

    def cot_copies(step, act):
        buf = lax.rem(step, 2)
        for k in range(subs):
            at = step * subs + k
            act(
                pltpu.make_async_copy(
                    cot.at[sslot[at], pl.ds(al(spos[at], SUB), SUB)],
                    cot_v.at[buf, pl.ds(k * SUB, SUB)],
                    sem_c.at[buf],
                )
            )

    @pl.when(b == 0)
    def _():
        cot_copies(b, lambda c: c.start())
        gwo[...] = jnp.zeros_like(gwo)
        gwi[...] = jnp.zeros_like(gwi)
        gwu[...] = jnp.zeros_like(gwu)
        gvec[...] = jnp.zeros_like(gvec)
        gbi[...] = jnp.zeros_like(gbi)

    @pl.when(b + 1 < nb)
    def _():
        cot_copies(b + 1, lambda c: c.start())

    bo, g1, s1, bu, g2, s2 = [vec[k : k + 1, :] for k in range(6)]
    x = rows[...].astype(F32)
    c = ctx[...]
    n1, sc1 = norm(x + (dot(c, wo[...]) + bo))
    mixed = n1 * g1 + s1
    low = mixed.astype(BF16)

    def forward(k, branch):
        at = pl.ds(al(k * D, D), D)
        inner = dot(low, wi[:, at]) + bi[:, at]
        half = 0.5 + 0.5 * lax.erf(inner * (0.5**0.5))
        act = (inner * half).astype(BF16)
        act_v[:, at] = act
        dg_v[:, at] = half + inner * (jnp.exp2(inner * inner * (-0.5 * LOG2E)) * (1.0 / math.sqrt(2 * math.pi)))
        return branch + dot(act, wu[at, :])

    branch = lax.fori_loop(0, FF // D, forward, jnp.zeros((B, D), F32))
    n2, sc2 = norm(mixed + (branch + bu))
    keep = live_mask(live, b)
    out_v[...] = jnp.where(keep, n2 * g2 + s2, 0.0).astype(BF16)

    def out_copies(act):
        for k in range(subs):
            at = b * subs + k

            @pl.when(live[at] > 0)
            def _(k=k, at=at):
                act(
                    pltpu.make_async_copy(
                        out_v.at[pl.ds(k * SUB, SUB)],
                        out_o.at[sslot[at], pl.ds(al(spos[at], SUB), SUB)],
                        sem_o,
                    )
                )

    out_copies(lambda cp: cp.start())
    cot_copies(b, lambda cp: cp.wait())
    go = jnp.where(keep, cot_v[lax.rem(b, 2)].astype(F32), 0.0)
    gvec[4:5, :] += jnp.sum(go * n2, axis=0, keepdims=True)
    gvec[5:6, :] += jnp.sum(go, axis=0, keepdims=True)
    gs = norm_back(go * g2, n2, sc2)
    gb = gs.astype(BF16)
    gvec[3:4, :] += jnp.sum(gb.astype(F32), axis=0, keepdims=True)

    def backward(k, gm):
        at = pl.ds(al(k * D, D), D)
        gi = (dot_nt(gb, wu[at, :]) * dg_v[:, at]).astype(BF16)
        gbi[:, at] += jnp.sum(gi.astype(F32), axis=0, keepdims=True)
        gwu[at, :] += dot_tn(act_v[:, at], gb)
        gwi[:, at] += dot_tn(low, gi)
        return gm + dot_nt(gi, wi[:, at])

    gm = lax.fori_loop(0, FF // D, backward, gs)
    gvec[1:2, :] += jnp.sum(gm * n1, axis=0, keepdims=True)
    gvec[2:3, :] += jnp.sum(gm, axis=0, keepdims=True)
    ga = norm_back(gm * g1, n1, sc1).astype(BF16)
    ga_o[...] = ga
    gvec[0:1, :] += jnp.sum(ga.astype(F32), axis=0, keepdims=True)
    gwo[...] += dot_tn(c, ga)
    gc = dot_nt(ga, wo[...]).astype(BF16)
    gc_o[...] = gc
    prod = gc.astype(F32) * c.astype(F32)
    high = prod.astype(BF16)
    rest = (prod - high.astype(F32)).astype(BF16)
    heads = (
        lax.broadcasted_iota(jnp.int32, (D, 128), 0) // 64 == lax.broadcasted_iota(jnp.int32, (D, 128), 1)
    ).astype(BF16)
    dd_o[...] = dot(high, heads) + dot(rest, heads)
    out_copies(lambda cp: cp.wait())

    @pl.when(b == nb - 1)
    def _():
        gvec_o[...] = gvec[...]
        gbi_o[...] = gbi[...]
        stage[0] = gwo[...].astype(BF16)
        copies = [pltpu.make_async_copy(stage.at[0], gwo_o, sem_w.at[0])]
        copies[0].start()
        for k in range(4):
            buf = (k + 1) % 2
            if k:
                copies[k - 1].wait()
            stage[buf] = gwu[k * D : (k + 1) * D, :].astype(BF16)
            copies.append(pltpu.make_async_copy(stage.at[buf], gwu_o.at[pl.ds(k * D, D)], sem_w.at[buf]))
            copies[-1].start()
        for k in range(4):
            buf = (k + 5) % 2
            copies[k + 3].wait()
            stage[buf] = gwi[:, k * D : (k + 1) * D].astype(BF16)
            copies.append(pltpu.make_async_copy(stage.at[buf], gwi_o.at[:, pl.ds(k * D, D)], sem_w.at[buf]))
            copies[-1].start()
        copies[-2].wait()
        copies[-1].wait()


def row_by_row(tot, sslot, spos, live, rows, ctx, cot, wo, wi, wu, vec, bi):
    def at(b, tot, *_):
        return (jnp.minimum(b, tot[1] - 1), 0)

    block = pl.BlockSpec((B, D), at)
    whole = pl.BlockSpec(memory_space=pltpu.VMEM)
    return pl.pallas_call(
        rows_kernel,
        grid_spec=pltpu.PrefetchScalarGridSpec(
            num_scalar_prefetch=4,
            grid=(RP // B,),
            in_specs=[block, block, ANY, whole, whole, whole, whole, whole],
            out_specs=[ANY, block, block, pl.BlockSpec((B, 128), at), ANY, ANY, ANY, whole, whole],
            scratch_shapes=[
                pltpu.VMEM((2, B, D), BF16),
                pltpu.VMEM((B, D), BF16),
                pltpu.VMEM((B, FF), BF16),
                pltpu.VMEM((B, FF), F32),
                pltpu.VMEM((D, D), F32),
                pltpu.VMEM((D, FF), F32),
                pltpu.VMEM((FF, D), F32),
                pltpu.VMEM((8, D), F32),
                pltpu.VMEM((1, FF), F32),
                pltpu.VMEM((2, D, D), BF16),
                pltpu.SemaphoreType.DMA((2,)),
                pltpu.SemaphoreType.DMA,
                pltpu.SemaphoreType.DMA((2,)),
            ],
        ),
        out_shape=[
            jax.ShapeDtypeStruct((SLOTS, T, D), BF16),
            jax.ShapeDtypeStruct((RP, D), BF16),
            jax.ShapeDtypeStruct((RP, D), BF16),
            jax.ShapeDtypeStruct((RP, 128), F32),
            jax.ShapeDtypeStruct((D, D), BF16),
            jax.ShapeDtypeStruct((D, FF), BF16),
            jax.ShapeDtypeStruct((FF, D), BF16),
            jax.ShapeDtypeStruct((8, D), F32),
            jax.ShapeDtypeStruct((1, FF), F32),
        ],
        compiler_params=pltpu.CompilerParams(
            vmem_limit_bytes=60 << 20, dimension_semantics=("arbitrary",)
        ),
        name="row_by_row",
    )(tot, sslot, spos, live, rows, ctx, cot, wo, wi, wu, vec, bi)


def back_kernel(
    lens, offs, tot, sslot, spos, live, rows, qkv, gc, ga, lse, dd, w,
    gin_o, gw_o, gb_o,
    rows_v, qkv_v, gc_v, ga_v, lse_v, dd_v, dk, dv, gw, gb, gin_v, stage, sem_in, sem_g, sem_w,
):
    blocks = tot[1]
    arrays = ((qkv, qkv_v), (gc, gc_v), (lse, lse_v), (dd, dd_v), (rows, rows_v), (ga, ga_v))

    def loads(b, act):
        at = pl.ds(al(b * B, B), B)
        for k, (hbm, vmem) in enumerate(arrays):
            act(pltpu.make_async_copy(hbm.at[at], vmem.at[at], sem_in.at[k]))

    def start_load(b, _):
        loads(b, lambda c: c.start())
        return 0

    def wait_load(b, _):
        loads(b, lambda c: c.wait())
        return 0

    lax.fori_loop(0, blocks, start_load, 0)
    qkv_v[pl.ds(al(blocks * B, B), B), :] = jnp.zeros((B, WIDE), BF16)
    tail = pl.ds(al(blocks * B, B), B)
    gc_v[tail, :] = jnp.zeros((B, D), BF16)
    lse_v[tail, :] = jnp.zeros((B, 128), F32)
    dd_v[tail, :] = jnp.zeros((B, 128), F32)
    gw[...] = jnp.zeros_like(gw)
    gb[...] = jnp.zeros_like(gb)
    lax.fori_loop(0, blocks, wait_load, 0)

    lane = lax.broadcasted_iota(jnp.int32, (B, 128), 1)
    row = lax.broadcasted_iota(jnp.int32, (B, 128), 0)
    key_row = lax.broadcasted_iota(jnp.int32, (B, B), 0)

    def sequence(s, _):
        length = lens[s]
        off = offs[s]
        spans = (length + B - 1) // B

        def pair(p, t):
            c0 = al(p * 128, 128)
            kc = pl.ds(al(D + p * 128, 128), 128)
            vc = pl.ds(al(2 * D + p * 128, 128), 128)
            for j in range(t):
                dk[j] = jnp.zeros((B, 128), F32)
                dv[j] = jnp.zeros((B, 128), F32)

            def query_block(q, _):
                r0 = al(off + q * B, SUB)
                at = pl.ds(r0, B)
                qp = qkv_v[at, pl.ds(c0, 128)]
                fresh = row < length - q * B
                gp = jnp.where(fresh, gc_v[at, pl.ds(c0, 128)], jnp.zeros((B, 128), BF16))
                lse_t = jnp.transpose(lse_v[at, :])
                dd_t = jnp.transpose(jnp.where(fresh, dd_v[at, :], 0.0))
                head = lax.broadcasted_iota(jnp.int32, (128, B), 0)
                dq = jnp.zeros((B, 128), F32)
                for h in range(2):
                    half = (lane < 64) if h == 0 else (lane >= 64)
                    qm = jnp.where(half, qp, jnp.zeros_like(qp))
                    gm = jnp.where(half, gp, jnp.zeros_like(gp))
                    mine = head == 2 * p + h
                    lse_h = jnp.sum(jnp.where(mine, lse_t, 0.0), axis=0, keepdims=True)
                    dd_h = jnp.sum(jnp.where(mine, dd_t, 0.0), axis=0, keepdims=True)
                    for j in range(t):
                        kat = pl.ds(al(off + j * B, SUB), B)
                        k = qkv_v[kat, kc]
                        v = qkv_v[kat, vc]
                        pt = jnp.exp2(dot_nt(k, qm) * SC2 - lse_h)
                        if j == t - 1:
                            pt = jnp.where(key_row < length - j * B, pt, 0.0)
                        dv[j] += dot(pt.astype(BF16), gm)
                        ds = (pt * (dot_nt(v, gm) - dd_h)).astype(BF16)
                        dk[j] += dot(ds, qm)
                        dq += dot_tn(ds, jnp.where(half, k, jnp.zeros_like(k)))
                qkv_v[at, pl.ds(c0, 128)] = jnp.where(fresh, (dq * SCALE).astype(BF16), qp)
                return 0

            lax.fori_loop(0, spans, query_block, 0)
            for j in range(t):
                kat = pl.ds(al(off + j * B, SUB), B)
                fresh = row < length - j * B
                qkv_v[kat, kc] = jnp.where(fresh, (dk[j] * SCALE).astype(BF16), qkv_v[kat, kc])
                qkv_v[kat, vc] = jnp.where(fresh, dv[j].astype(BF16), qkv_v[kat, vc])

        def pairs(p, _):
            for t in range(1, T // B + 1):

                @pl.when(spans == t)
                def _(t=t):
                    pair(p, t)

            return 0

        lax.fori_loop(0, HEADS // 2, pairs, 0)
        return 0

    lax.fori_loop(0, SLOTS, sequence, 0)
    subs = B // SUB

    def gin_copies(b, act):
        for k in range(subs):
            at = b * subs + k

            @pl.when(live[at] > 0)
            def _(k=k, at=at):
                act(
                    pltpu.make_async_copy(
                        gin_v.at[lax.rem(b, 2), pl.ds(k * SUB, SUB)],
                        gin_o.at[sslot[at], pl.ds(al(spos[at], SUB), SUB)],
                        sem_g.at[lax.rem(b, 2)],
                    )
                )

    def gather(b, _):
        at = pl.ds(al(b * B, B), B)
        keep = live_mask(live, b)
        x = rows_v[at, :]
        total = ga_v[at, :].astype(F32)
        for part in range(3):
            cols = slice(part * D, (part + 1) * D)
            g = jnp.where(keep, qkv_v[at, cols], jnp.zeros((B, D), BF16))
            gb[:, cols] += jnp.sum(g.astype(F32), axis=0, keepdims=True)
            gw[:, cols] += dot_tn(x, g)
            total = total + dot_nt(g, w[:, cols])

        @pl.when(b >= 2)
        def _():
            gin_copies(b - 2, lambda c: c.wait())

        gin_v[lax.rem(b, 2)] = total.astype(BF16)
        gin_copies(b, lambda c: c.start())
        return 0

    lax.fori_loop(0, blocks, gather, 0)
    gb_o[...] = gb[...]
    copies = []
    for part in range(3):
        if part >= 2:
            copies[part - 2].wait()
        cols = slice(part * D, (part + 1) * D)
        stage[part % 2] = gw[:, cols].astype(BF16)
        copies.append(pltpu.make_async_copy(stage.at[part % 2], gw_o.at[part], sem_w.at[part % 2]))
        copies[-1].start()
    for c in copies[1:]:
        c.wait()

    def last(b, _):
        gin_copies(b, lambda c: c.wait())
        return 0

    lax.fori_loop(jnp.maximum(blocks - 2, 0), blocks, last, 0)


def attend_back(lens, offs, tot, sslot, spos, live, rows, qkv, gc, ga, lse, dd, w):
    whole = pl.BlockSpec(memory_space=pltpu.VMEM)
    return pl.pallas_call(
        back_kernel,
        grid_spec=pltpu.PrefetchScalarGridSpec(
            num_scalar_prefetch=6,
            grid=(),
            in_specs=[ANY] * 6 + [whole],
            out_specs=[ANY, ANY, whole],
            scratch_shapes=[
                pltpu.VMEM((RP, D), BF16),
                pltpu.VMEM((RP, WIDE), BF16),
                pltpu.VMEM((RP, D), BF16),
                pltpu.VMEM((RP, D), BF16),
                pltpu.VMEM((RP, 128), F32),
                pltpu.VMEM((RP, 128), F32),
                pltpu.VMEM((T // B, B, 128), F32),
                pltpu.VMEM((T // B, B, 128), F32),
                pltpu.VMEM((D, WIDE), F32),
                pltpu.VMEM((1, WIDE), F32),
                pltpu.VMEM((2, B, D), BF16),
                pltpu.VMEM((2, D, D), BF16),
                pltpu.SemaphoreType.DMA((6,)),
                pltpu.SemaphoreType.DMA((2,)),
                pltpu.SemaphoreType.DMA((2,)),
            ],
        ),
        out_shape=[
            jax.ShapeDtypeStruct((SLOTS, T, D), BF16),
            jax.ShapeDtypeStruct((3, D, D), BF16),
            jax.ShapeDtypeStruct((1, WIDE), F32),
        ],
        compiler_params=pltpu.CompilerParams(vmem_limit_bytes=60 << 20),
        name="attend_back",
    )(lens, offs, tot, sslot, spos, live, rows, qkv, gc, ga, lse, dd, w)


def plan(lengths, order, n, me):
    nseq = lengths.shape[0]
    quarter = n // 4
    ids = lax.iota(jnp.int32, nseq)
    ahead = (lengths[None, :] > lengths[:, None]) | (
        (lengths[None, :] == lengths[:, None]) & (ids[None, :] < ids[:, None])
    )
    rank = jnp.sum(ahead.astype(jnp.int32), axis=1)
    rank_of_slot = jnp.sum(jnp.where(order[:, None] == ids[None, :], rank[None, :], 0), axis=1)
    is_rank = rank[None, :] == ids[:, None]
    seq_of_rank = jnp.sum(jnp.where(is_rank, ids[None, :], 0), axis=1)
    len_of_rank = jnp.sum(jnp.where(is_rank, lengths[None, :], 0), axis=1)
    slot_of_rank = jnp.sum(jnp.where(rank_of_slot[None, :] == ids[:, None], ids[None, :], 0), axis=1)
    len_of_slot = jnp.sum(jnp.where(order[:, None] == ids[None, :], lengths[None, :], 0), axis=1)

    group = ids // quarter
    i = ids % quarter
    dev = jnp.zeros_like(ids)
    slot = jnp.zeros_like(ids)
    for g in range(8):
        dev = jnp.where(group == g, group_device(g, i, quarter), dev)
        slot = jnp.where(group == g, GROUP_SLOT[g], slot)
    mine = (dev == me)[None, :] & (slot[None, :] == lax.iota(jnp.int32, SLOTS)[:, None])
    lens = jnp.sum(jnp.where(mine, len_of_rank[None, :], 0), axis=1)
    subs = (lens + SUB - 1) // SUB
    ends = jnp.sum(
        jnp.where(lax.iota(jnp.int32, SLOTS)[None, :] <= lax.iota(jnp.int32, SLOTS)[:, None], subs[None, :], 0), axis=1
    )
    starts = ends - subs
    total = ends[SLOTS - 1] * SUB
    blocks = (total + B - 1) // B
    k = lax.iota(jnp.int32, RP // SUB)
    inside = (k[:, None] >= starts[None, :]) & (k[:, None] < ends[None, :])
    sslot = jnp.sum(jnp.where(inside, lax.iota(jnp.int32, SLOTS)[None, :], 0), axis=1)
    spos = jnp.sum(jnp.where(inside, (k[:, None] - starts[None, :]) * SUB, 0), axis=1)
    left = jnp.sum(jnp.where(inside, lens[None, :], 0), axis=1)
    live = jnp.clip(left - spos, 0, SUB)

    def fits(caps):
        good = None
        for g in range(8):
            ok = len_of_rank[g * quarter] <= caps[g] * (T // 4)
            good = ok if good is None else good & ok
        return good

    way = jnp.where(fits(CAPS[0]), 0, jnp.where(fits(CAPS[1]), 1, 2)).astype(jnp.int32)
    return dict(
        seq_of_rank=seq_of_rank, slot_of_rank=slot_of_rank, rank_of_slot=rank_of_slot, len_of_slot=len_of_slot,
        lens=lens, offs=starts * SUB, tot=jnp.stack([total, blocks]), sslot=sslot, spos=spos, live=live, way=way,
    )


def body(
    tokens, cotangent, lengths, order, query_weight, query_bias, key_weight, value_weight, value_bias,
    output_weight, output_bias, first_gain, first_shift, inner_weight, inner_bias, outer_weight, outer_bias,
    second_gain, second_shift,
):
    n = lax.axis_size("dp")
    me = lax.axis_index("dp")
    nseq, rows = tokens.shape[:2]
    dr = D // n
    fr = FF // n

    small = [query_bias, value_bias, output_bias, first_gain, first_shift, outer_bias, second_gain, second_shift]
    flat = jnp.concatenate(small + [inner_bias])
    flat = jnp.pad(flat, (0, 8 * D - flat.shape[0])).reshape(8, D)
    inner4 = inner_weight.reshape(dr, 4, D).transpose(1, 0, 2).reshape(4 * dr, D)
    shard = jnp.concatenate([query_weight, key_weight, value_weight, output_weight, inner4, outer_weight, flat], axis=0)
    full = lax.all_gather(shard, "dp", axis=0, tiled=False)

    p = plan(lengths, order, n, me)
    sorted_tokens, sorted_cot = sort_blocks(p["seq_of_rank"], p["slot_of_rank"], tokens, cotangent)

    def dealt(x, first_id):
        return lax.switch(
            p["way"],
            [functools.partial(deal, n=n, caps=CAPS[k], collective_id=first_id + k) for k in range(3)],
            x,
        )

    def collected(x, first_id):
        return lax.switch(
            p["way"],
            [
                functools.partial(collect, n=n, nseq=nseq, rows=rows, caps=CAPS[k], collective_id=first_id + k)
                for k in range(3)
            ],
            x,
        )

    x_in = dealt(sorted_tokens, 0)
    g_in = dealt(sorted_cot, 3)

    def part(lo, count):
        return full[:, lo : lo + count].reshape(n * count, D)

    wq, wk, wv, wo = [part(k * dr, dr) for k in range(4)]
    wi = full[:, 4 * dr : 8 * dr].reshape(n, 4, dr, D).transpose(0, 2, 1, 3).reshape(D, FF)
    wu = part(8 * dr, fr)
    vecs = full[:, 8 * dr + fr :].reshape(n, 8 * D)
    bq, bv, bo, g1, s1, bu, g2, s2 = [vecs[:, k * dr : (k + 1) * dr].reshape(D).astype(F32) for k in range(8)]
    bi = vecs[:, 8 * dr : 8 * dr + fr].reshape(1, FF).astype(F32)
    wqkv = jnp.concatenate([wq, wk, wv], axis=1)
    bqkv = jnp.concatenate([bq, jnp.zeros((D,), F32), bv]).reshape(1, WIDE)
    zero = jnp.zeros((D,), F32)
    vec = jnp.stack([bo, g1, s1, bu, g2, s2, zero, zero])

    packed, qkv, ctx, lse = attend(p["lens"], p["offs"], p["tot"], x_in, wqkv, bqkv)
    out, ga, gc, dd, gwo, gwi, gwu, gvec, gbi = row_by_row(
        p["tot"], p["sslot"], p["spos"], p["live"], packed, ctx, g_in, wo, wi, wu, vec, bi
    )
    y_out = collected(out, 6)
    gin, gqkv, gbqkv = attend_back(
        p["lens"], p["offs"], p["tot"], p["sslot"], p["spos"], p["live"], packed, qkv, gc, ga, lse, dd, wqkv
    )
    y_gin = collected(gin, 9)

    live_here = p["len_of_slot"] - me * rows
    output = unsort_blocks(p["rank_of_slot"], live_here, y_out)
    input_gradient = unsort_blocks(p["rank_of_slot"], live_here, y_gin)

    gq, gk, gv = [gqkv[k].reshape(n, dr, D) for k in range(3)]
    inner_piece = gwi.reshape(n, dr, 4, D).transpose(0, 2, 1, 3).reshape(n, 4 * dr, D)
    vectors = [gbqkv[0, :D], gbqkv[0, 2 * D :], gvec[0], gvec[1], gvec[2], gvec[3], gvec[4], gvec[5]]
    vec_piece = jnp.concatenate([v.reshape(n, dr) for v in vectors] + [gbi.reshape(n, fr)], axis=1).astype(BF16)
    vec_piece = jnp.pad(vec_piece, ((0, 0), (0, 8 * D - vec_piece.shape[1]))).reshape(n, 8, D)
    pieces = jnp.concatenate(
        [gq, gk, gv, gwo.reshape(n, dr, D), inner_piece, gwu.reshape(n, fr, D), vec_piece], axis=1
    )
    summed = lax.psum_scatter(pieces, "dp", scatter_dimension=0, tiled=False).astype(F32)
    sq, sk, sv, so = [summed[k * dr : (k + 1) * dr] for k in range(4)]
    si = summed[4 * dr : 8 * dr].reshape(4, dr, D).transpose(1, 0, 2).reshape(dr, FF)
    su = summed[8 * dr : 8 * dr + fr]
    svec = summed[8 * dr + fr :].reshape(8 * D)
    v = [svec[k * dr : (k + 1) * dr] for k in range(8)]
    sbi = svec[8 * dr : 8 * dr + fr]
    return (
        output, input_gradient, sq, v[0], sk, sv, v[1], so, v[2], v[3], v[4], si, sbi, su, v[5], v[6], v[7],
    )


def solution(mesh):
    matrix, vector = P("dp", None), P("dp")
    token = P(None, "dp", None)
    in_specs = (
        token, token, P(), P(), matrix, vector, matrix, matrix, vector, matrix, vector, vector, vector,
        matrix, vector, matrix, vector, vector, vector,
    )
    out_specs = (
        token, token, matrix, vector, matrix, matrix, vector, matrix, vector, vector, vector,
        matrix, vector, matrix, vector, vector, vector,
    )
    return jax.shard_map(body, mesh=mesh, in_specs=in_specs, out_specs=out_specs, check_vma=False)
```
